32 devices in a mesh: grp: 4 (over y, core), row: 8 (over z, x).
Axes of the slice: x: 2, y: 2, z: 4, core: 2. Of those that a mesh axis runs over, the one named last changes fastest.
Arguments:
- landmarks: bfloat16 [1024, 1024], P(('grp', 'row')), may hold values from -6.5 to 6.5
- initial_basis: bfloat16 [1024, 256], P(('grp', 'row')), may hold values from -0.1875 to 0.1875
- points: bfloat16 [32768, 1024], P(('grp', 'row')), may hold values from -6.5 to 6.5
Outputs:
- basis: float32 [1024, 256], P(('grp', 'row'))
- coords: float32 [32768, 256], P(('grp', 'row'))
The draws below stay inside these ranges and needn't reach their ends.
All inputs are finite; a program needn't handle non-finite values.
Results may differ from the reference program's by a relative error of at most 0.0057.
Values may be sent and summed in bfloat16 or wider, within the bound.
No kernel may reach another device: no remote copies, remote signals or barrier semaphores. Data moves between devices by JAX's collectives and lax.ppermute only.
A program may use at most 128 MiB of HBM per device.

```python
import math
import jax
import jax.numpy as jnp
from jax import lax

D = 1024
RANK = 256
ITERS = 2
L = 1024
NP = 32768


def cluster_rows(key, salt, count):
    centers = jax.random.truncated_normal(jax.random.fold_in(key, 11), -4.0, 4.0, (64, D), jnp.float32)
    member = jax.random.randint(jax.random.fold_in(key, salt), (count,), 0, 64)
    noise = 0.6 * jax.random.truncated_normal(jax.random.fold_in(key, salt + 1), -4.0, 4.0, (count, D), jnp.float32)
    return centers[member] + noise


def draw_landmarks(key, part):
    return cluster_rows(key, 21, L).astype(jnp.bfloat16)


def draw_points(key, part):
    return cluster_rows(key, 31, NP).astype(jnp.bfloat16)


def block_scale(stream_key, dims, shards, smallest, top_value):
    def one(dim, blocks):
        heights = jax.random.uniform(jax.random.fold_in(jax.random.fold_in(stream_key, 6), dim), (blocks,), jnp.float32, smallest / len(shards), top_value / len(shards))
        return jnp.repeat(jnp.exp(heights), dims[dim] // blocks).reshape((-1,) + (1,) * (len(dims) - dim - 1))

    loudness = one(*shards[0])
    for cut in shards[1:]:
        loudness = loudness * one(*cut)
    return loudness


def bell_draw(rng, shape, scale, most, split=(), dtype=jnp.bfloat16):
    level = block_scale(rng, shape, split, -0.22, 0.18) if split else 1.0
    drawn = jax.random.normal(rng, shape, jnp.float32) * scale * level
    return jnp.minimum(jnp.maximum(drawn, -most), most).astype(dtype)


def setup_inputs(seed: int = 0) -> dict:
    key_of = jax.random.split(jax.random.key(seed), 4)
    return {
        "landmarks": draw_landmarks(jax.random.fold_in(key_of[3], 71), 0),
        "initial_basis": bell_draw(key_of[1], (L, RANK), L ** -0.5, 0.1875, ((0, 32),)),
        "points": draw_points(jax.random.fold_in(key_of[3], 71), 0),
    }


spread = 0.25

def pair_kernel(left, right):
    left_sq = lax.optimization_barrier(jnp.sum(jnp.square(left.astype(jnp.float32)), axis=1))
    right_sq = lax.optimization_barrier(jnp.sum(jnp.square(right.astype(jnp.float32)), axis=1))
    inner = lax.dot_general(left.astype(jnp.float32), right.astype(jnp.float32), (((1,), (1,)), ((), ())), precision=lax.Precision.HIGHEST)
    dist = left_sq[:, None] + right_sq[None, :] - 2.0 * inner
    return jnp.exp(-dist / (spread * left.shape[1]))

def reference(landmarks, initial_basis, points):
    total = landmarks.shape[0]
    width = landmarks.shape[1]
    blocks = landmarks.reshape(4, total // 4, width)
    land_kernel = lax.map(lambda block: pair_kernel(block, landmarks), blocks).reshape(total, total)
    degree = lax.optimization_barrier(jnp.sum(land_kernel, axis=1))
    inverse_root = 1.0 / jnp.sqrt(degree)
    affinity = (land_kernel * inverse_root[:, None] * inverse_root[None, :]).astype(jnp.bfloat16)
    affinity = lax.optimization_barrier(affinity).astype(jnp.float32)
    current = initial_basis
    for step in range(ITERS):
        image = jnp.dot(affinity, current.astype(jnp.float32), precision=lax.Precision.HIGHEST)
        gram = jnp.dot(image.T, image, precision=lax.Precision.HIGHEST)
        lower = jnp.linalg.cholesky(gram)
        ortho = jax.scipy.linalg.solve_triangular(lower, image.T, lower=True).T
        current = ortho.astype(jnp.bfloat16)
    lam = jnp.diagonal(lower)
    spectral = (ortho * inverse_root[:, None] / lam[None, :]).astype(jnp.bfloat16)
    spectral = lax.optimization_barrier(spectral).astype(jnp.float32)
    count = points.shape[0]
    block_rows = min(512, count)
    root = math.sqrt(total)

    def embed(block):
        point_kernel = pair_kernel(block, landmarks)
        point_degree = lax.optimization_barrier(jnp.sum(point_kernel, axis=1))
        weights = lax.optimization_barrier(point_kernel.astype(jnp.bfloat16)).astype(jnp.float32)
        numer = jnp.dot(weights, spectral, precision=lax.Precision.HIGHEST)
        return numer / jnp.sqrt(point_degree)[:, None] * root
    coords = lax.map(embed, points.reshape(count // block_rows, block_rows, width)).reshape(count, -1)
    return (ortho, coords)
```

```python
import math

import jax
import jax.numpy as jnp
from jax import lax
from jax.sharding import PartitionSpec as P

ITERS = 2
AXES = ("grp", "row")

spread = 0.25


def squared_rows(rows):
    return jnp.sum(jnp.square(rows.astype(jnp.float32)), axis=1)


def pair_kernel(left, right):
    inner = lax.dot_general(
        left, right, (((1,), (1,)), ((), ())), preferred_element_type=jnp.float32
    )
    dist = squared_rows(left)[:, None] + squared_rows(right)[None, :] - 2.0 * inner
    return jnp.exp(-dist / (spread * left.shape[1]))


def exchange(value, mask):
    count = lax.axis_size("grp") * lax.axis_size("row")
    return lax.ppermute(value, AXES, [(i, i ^ mask) for i in range(count)])


def gather_relative(own):
    rows = lax.axis_size("row")
    near, partner, across = 1, rows, 2 * rows
    parts = [own] + [exchange(own, mask) for mask in range(2, rows, 2)]
    half = len(parts) // 2
    first = jnp.concatenate(parts[:half], axis=0)
    second = jnp.concatenate(parts[half:], axis=0)
    first_near = exchange(first, near)
    second_across = exchange(second, across)
    first_pair = jnp.concatenate([first, first_near], axis=0)
    second_pair = jnp.concatenate([second, second_across], axis=0)
    first_rest = exchange(first_pair, across)
    second_rest = exchange(second_pair, near)
    mine = jnp.concatenate([first_pair, second_pair, first_rest, second_rest], axis=0)
    return mine, exchange(mine, partner)


def fused_body(landmarks, initial_basis, points):
    local_rows, width = landmarks.shape
    own = jnp.concatenate([landmarks, initial_basis], axis=1)
    mine, theirs = gather_relative(own)
    both = jnp.concatenate([mine, theirs], axis=0)
    anchors, current = both[:, :width], both[:, width:]
    total = anchors.shape[0]
    land_kernel = pair_kernel(anchors, anchors)
    scale = lax.rsqrt(jnp.sum(land_kernel, axis=1))
    affinity = (land_kernel * scale[:, None] * scale[None, :]).astype(jnp.bfloat16)
    for step in range(ITERS):
        image = jnp.dot(affinity, current, preferred_element_type=jnp.float32)
        gram = jnp.dot(image.T, image, precision=lax.Precision.HIGHEST)
        lower = jnp.linalg.cholesky(gram)
        inverse = jax.scipy.linalg.solve_triangular(lower, jnp.eye(gram.shape[0], dtype=gram.dtype), lower=True)
        ortho = jnp.dot(image, inverse.T, precision=lax.Precision.HIGHEST)
        current = ortho.astype(jnp.bfloat16)
    lam = jnp.diagonal(lower)
    spectral = (ortho * scale[:, None] / lam[None, :]).astype(jnp.bfloat16)
    weights = pair_kernel(points, anchors)
    numer = jnp.dot(weights.astype(jnp.bfloat16), spectral, preferred_element_type=jnp.float32)
    coords = numer / jnp.sqrt(jnp.sum(weights, axis=1))[:, None] * math.sqrt(total)
    return (ortho[:local_rows], coords)


def body(landmarks, initial_basis, points):
    local_rows = landmarks.shape[0]
    total = local_rows * lax.axis_size("grp") * lax.axis_size("row")
    row_index = lax.axis_index("row")
    group_rows = lax.all_gather(landmarks, "row", axis=0, tiled=True)
    cross_rows = lax.all_gather(landmarks, "grp", axis=0, tiled=True)
    land_kernel = pair_kernel(group_rows, cross_rows)
    group_degree = lax.psum(jnp.sum(land_kernel, axis=1), "row")
    own_degree = lax.dynamic_slice_in_dim(group_degree, row_index * local_rows, local_rows, 0)
    cross_degree = lax.psum(jnp.sum(land_kernel, axis=0), "grp")
    row_scale = 1.0 / jnp.sqrt(group_degree)
    column_scale = 1.0 / jnp.sqrt(cross_degree)
    affinity = (land_kernel * row_scale[:, None] * column_scale[None, :]).astype(jnp.bfloat16)
    current = initial_basis
    for step in range(ITERS):
        cross_basis = lax.all_gather(current, "grp", axis=0, tiled=True)
        image = lax.psum_scatter(
            jnp.dot(affinity, cross_basis, preferred_element_type=jnp.float32),
            "row",
            scatter_dimension=0,
            tiled=True,
        )
        gram = lax.psum(jnp.dot(image.T, image, precision=lax.Precision.HIGHEST), ("grp", "row"))
        lower = jnp.linalg.cholesky(gram)
        ortho = jax.scipy.linalg.solve_triangular(lower, image.T, lower=True).T
        current = ortho.astype(jnp.bfloat16)
    lam = jnp.diagonal(lower)
    own_scale = 1.0 / jnp.sqrt(own_degree)
    spectral = (ortho * own_scale[:, None] / lam[None, :]).astype(jnp.bfloat16)
    anchors = lax.all_gather(landmarks, AXES, axis=0, tiled=True)
    all_spectral = lax.all_gather(spectral, AXES, axis=0, tiled=True)
    weights = pair_kernel(points, anchors)
    numer = jnp.dot(weights.astype(jnp.bfloat16), all_spectral, preferred_element_type=jnp.float32)
    coords = numer / jnp.sqrt(jnp.sum(weights, axis=1))[:, None] * math.sqrt(total)
    return (ortho, coords)


REDUNDANT_BYTES = 8 * 2**20


def solution(mesh):
    sizes = dict(mesh.shape)
    rows = sizes["row"]

    def run(landmarks, initial_basis, points):
        total = landmarks.shape[0]
        fits = 4 * total * total <= REDUNDANT_BYTES
        cube = sizes["grp"] == 4 and rows >= 4 and rows & (rows - 1) == 0
        spec = P(AXES, None)
        inner = jax.shard_map(
            fused_body if fits and cube else body,
            mesh=mesh,
            in_specs=(spec, spec, spec),
            out_specs=(spec, spec),
            check_vma=False,
        )
        return inner(landmarks, initial_basis, points)

    return run
```

```python
import functools
import math

import jax
import jax.numpy as jnp
from jax import lax
from jax.experimental import pallas as pl
from jax.experimental.pallas import tpu as pltpu
from jax.sharding import PartitionSpec as P

ITERS = 2
AXES = ("grp", "row")
spread = 0.25
LANES = 128
NN = (((1,), (0,)), ((), ()))
NT = (((1,), (1,)), ((), ()))
TN = (((0,), (0,)), ((), ()))
F32 = jnp.float32
BF16 = jnp.bfloat16


def mm(a, b, dims):
    return lax.dot_general(a, b, dims, preferred_element_type=F32)


def split(x):
    high = x.astype(BF16)
    return high, (x - high.astype(F32)).astype(BF16)


def mm_split(a, b, dims):
    return mm(a[0], b[0], dims) + (mm(a[0], b[1], dims) + mm(a[1], b[0], dims))


def square_iota(n):
    return lax.broadcasted_iota(jnp.int32, (n, n), 0), lax.broadcasted_iota(jnp.int32, (n, n), 1)


def column_to_row(column):
    n = column.shape[0]
    i, j = square_iota(LANES)
    pieces = []
    for at in range(0, n, LANES):
        pieces.append(jnp.sum(jnp.where(i == j, column[at : at + LANES], 0.0), axis=0, keepdims=True))
    return jnp.concatenate(pieces, axis=1)


def direct_inverse(gram, work, unit):
    n = gram.shape[0]
    i, j = square_iota(n)
    row_at = lax.broadcasted_iota(jnp.int32, (n, 1), 0)
    work[...] = gram
    unit[...] = jnp.where(i == j, 1.0, 0.0)

    def step(k, pivots):
        row = work[pl.ds(k, 1), :]
        column = jnp.sum(jnp.where(j == k, work[...], 0.0), axis=1, keepdims=True)
        pivot = jnp.sum(jnp.where(row_at == k, column, 0.0), axis=0, keepdims=True)
        factor = jnp.where(row_at > k, column / pivot, 0.0)
        work[...] = work[...] - factor * row
        unit[...] = unit[...] - factor * unit[pl.ds(k, 1), :]
        return jnp.where(row_at == k, pivot, pivots)

    pivots = lax.fori_loop(0, n, step, jnp.ones((n, 1), F32))
    unit[...] = unit[...] / jnp.sqrt(pivots)


TOLERANCE = 0.05
STEPS = 5
MORE = 16


def factor_inverse(gram, out, work, corr):
    n = gram.shape[0]
    i, j = square_iota(n)
    eye = jnp.where(i == j, 1.0, 0.0)
    half = jnp.where(i > j, 1.0, 0.5 * eye)
    diagonal = jnp.where(i == j, gram, 0.0)
    row_scale = lax.rsqrt(jnp.sum(diagonal, axis=0, keepdims=True))
    column_scale = lax.rsqrt(jnp.sum(diagonal, axis=1, keepdims=True))
    start = gram * column_scale * row_scale
    pair = split(start)
    state, inverse = start, eye
    for step in range(STEPS):
        change = (state - eye) * half
        low = change.astype(BF16)
        if step < STEPS - 1:
            left = state - mm(low, state.astype(BF16), NN)
            state = left - mm(left.astype(BF16), low, NT)
        inverse = eye - change if step == 0 else inverse - mm(low, inverse.astype(BF16), NN)

    def polish(inverse, parts):
        mine = split(inverse)
        state = mm_split(split(mm_split(mine, parts, NN)), mine, NT)
        error = state - eye
        change = (error * half).astype(BF16)
        better = inverse - mm(change, inverse.astype(BF16), NN)
        signs = jnp.where(jnp.logical_and(i == j, better <= 0.0), 1.0, 0.0)
        return better, jnp.sum(error * error + signs)

    inverse, error = polish(inverse, pair)
    out[...] = inverse * row_scale

    @pl.when(jnp.logical_not(error < TOLERANCE**2))
    def _():
        corr[...] = start
        work[...] = inverse

        def again(carry):
            count, _ = carry
            better, error = polish(work[...], split(corr[...]))
            work[...] = better
            return count + 1, error

        def more(carry):
            count, error = carry
            return jnp.logical_and(count < MORE, jnp.logical_not(error < TOLERANCE**2))

        _, last = lax.while_loop(more, again, (0, error))
        out[...] = work[...] * row_scale

        @pl.when(jnp.logical_not(last < TOLERANCE**2))
        def _():
            direct_inverse(corr[...], work, out)
            out[...] = out[...] * row_scale


def chunked(total, size, body):
    count = total // size
    if count == 1:
        body(0)
    else:
        lax.fori_loop(0, count, lambda c, _: (body(pl.multiple_of(c * size, size)), 0)[1], 0)


def row_squares(rows):
    wide = rows.astype(F32)
    return jnp.sum(wide * wide, axis=1, keepdims=True)


def stage_kernel(local_rows, chunk, mine, theirs, points, ortho_out, coords_out,
                 anchors, basis, kernel, affinity, weights, degree_p, image, inverse, work, corr):
    width = points.shape[1]
    half_rows = mine.shape[0]
    total = 2 * half_rows
    rate = math.log2(math.e) / (spread * width)
    anchors[0:half_rows, :] = mine[:, :width]
    anchors[half_rows:total, :] = theirs[:, :width]
    basis[0:half_rows, :] = mine[:, width:]
    basis[half_rows:total, :] = theirs[:, width:]
    squares = jnp.concatenate([row_squares(anchors[at : at + chunk, :]) for at in range(0, total, chunk)], axis=0) * rate
    squares_row = column_to_row(squares)
    sums = []
    for at in range(0, total, chunk):
        inner = mm(anchors[at : at + chunk, :], anchors[...], NT)
        value = jnp.exp2(inner * (2.0 * rate) - squares[at : at + chunk] - squares_row)
        kernel[at : at + chunk, :] = value
        sums.append(jnp.sum(value, axis=1, keepdims=True))
    scale = lax.rsqrt(jnp.concatenate(sums, axis=0))
    scale_row = column_to_row(scale)
    for at in range(0, total, chunk):
        affinity[at : at + chunk, :] = (kernel[at : at + chunk, :] * scale[at : at + chunk] * scale_row).astype(BF16)
    for step in range(ITERS):
        if step == 0:
            value = mm(basis[...], affinity[...], TN)
        else:
            value = mm(current, affinity[...], NN)
        parts = split(value)
        gram = mm_split(parts, parts, NT)
        factor_inverse(gram, inverse, work, corr)
        ortho = mm_split(split(inverse[...]), parts, NN)
        current = ortho.astype(BF16)
    i, j = square_iota(inverse.shape[0])
    reciprocal = jnp.sum(jnp.where(i == j, inverse[...], 0.0), axis=1, keepdims=True)
    spectral = (ortho * scale_row * reciprocal).astype(BF16)
    lanes = -(-local_rows // LANES) * LANES
    ortho_out[...] = jnp.transpose(ortho[:, 0:lanes])[0:local_rows, :]
    image[...] = spectral

    for at in range(0, points.shape[0], chunk):
        block = points[at : at + chunk, :]
        inner = mm(block, anchors[...], NT)
        value = jnp.exp2(inner * (2.0 * rate) - row_squares(block) * rate - squares_row)
        degree = jnp.sum(value, axis=1, keepdims=True)
        numer = mm(value.astype(BF16), image[...], NT)
        coords_out[at : at + chunk, :] = numer * (lax.rsqrt(degree) * math.sqrt(total))


def stage(local_rows, mine, theirs, points):
    half_rows, wide = mine.shape
    count, width = points.shape
    rank = wide - width
    total = 2 * half_rows
    chunk = 256
    vmem = pl.BlockSpec(memory_space=pltpu.VMEM)
    return pl.pallas_call(
        functools.partial(stage_kernel, local_rows, chunk),
        out_shape=(jax.ShapeDtypeStruct((local_rows, rank), F32), jax.ShapeDtypeStruct((count, rank), F32)),
        in_specs=[vmem] * 3,
        out_specs=(vmem, vmem),
        scratch_shapes=[
            pltpu.VMEM((total, width), BF16),
            pltpu.VMEM((total, rank), BF16),
            pltpu.VMEM((total, total), F32),
            pltpu.VMEM((total, total), BF16),
            pltpu.VMEM((8, LANES), F32),
            pltpu.VMEM((8, LANES), F32),
            pltpu.VMEM((rank, total), BF16),
            pltpu.VMEM((rank, rank), F32),
            pltpu.VMEM((rank, rank), F32),
            pltpu.VMEM((rank, rank), F32),
        ],
        compiler_params=pltpu.CompilerParams(vmem_limit_bytes=56 * 2**20),
    )(mine, theirs, points)


def squared_rows(rows):
    return jnp.sum(jnp.square(rows.astype(jnp.float32)), axis=1)


def pair_kernel(left, right):
    inner = lax.dot_general(
        left, right, (((1,), (1,)), ((), ())), preferred_element_type=jnp.float32
    )
    dist = squared_rows(left)[:, None] + squared_rows(right)[None, :] - 2.0 * inner
    return jnp.exp(-dist / (spread * left.shape[1]))


def exchange(value, mask):
    count = lax.axis_size("grp") * lax.axis_size("row")
    return lax.ppermute(value, AXES, [(i, i ^ mask) for i in range(count)])


def gather_relative(own):
    rows = lax.axis_size("row")
    near, partner, across = 1, rows, 2 * rows
    parts = [own] + [exchange(own, mask) for mask in range(2, rows, 2)]
    half = len(parts) // 2
    first = jnp.concatenate(parts[:half], axis=0)
    second = jnp.concatenate(parts[half:], axis=0)
    first_near = exchange(first, near)
    second_across = exchange(second, across)
    first_pair = jnp.concatenate([first, first_near], axis=0)
    second_pair = jnp.concatenate([second, second_across], axis=0)
    first_rest = exchange(first_pair, across)
    second_rest = exchange(second_pair, near)
    mine = jnp.concatenate([first_pair, second_pair, first_rest, second_rest], axis=0)
    return mine, exchange(mine, partner)


def fused_body(landmarks, initial_basis, points):
    own = jnp.concatenate([landmarks, initial_basis], axis=1)
    mine, theirs = gather_relative(own)
    return stage(landmarks.shape[0], mine, theirs, points)


def body(landmarks, initial_basis, points):
    local_rows = landmarks.shape[0]
    total = local_rows * lax.axis_size("grp") * lax.axis_size("row")
    row_index = lax.axis_index("row")
    group_rows = lax.all_gather(landmarks, "row", axis=0, tiled=True)
    cross_rows = lax.all_gather(landmarks, "grp", axis=0, tiled=True)
    land_kernel = pair_kernel(group_rows, cross_rows)
    group_degree = lax.psum(jnp.sum(land_kernel, axis=1), "row")
    own_degree = lax.dynamic_slice_in_dim(group_degree, row_index * local_rows, local_rows, 0)
    cross_degree = lax.psum(jnp.sum(land_kernel, axis=0), "grp")
    row_scale = 1.0 / jnp.sqrt(group_degree)
    column_scale = 1.0 / jnp.sqrt(cross_degree)
    affinity = (land_kernel * row_scale[:, None] * column_scale[None, :]).astype(jnp.bfloat16)
    current = initial_basis
    for step in range(ITERS):
        cross_basis = lax.all_gather(current, "grp", axis=0, tiled=True)
        image = lax.psum_scatter(
            jnp.dot(affinity, cross_basis, preferred_element_type=jnp.float32),
            "row",
            scatter_dimension=0,
            tiled=True,
        )
        gram = lax.psum(jnp.dot(image.T, image, precision=lax.Precision.HIGHEST), ("grp", "row"))
        lower = jnp.linalg.cholesky(gram)
        ortho = jax.scipy.linalg.solve_triangular(lower, image.T, lower=True).T
        current = ortho.astype(jnp.bfloat16)
    lam = jnp.diagonal(lower)
    own_scale = 1.0 / jnp.sqrt(own_degree)
    spectral = (ortho * own_scale[:, None] / lam[None, :]).astype(jnp.bfloat16)
    anchors = lax.all_gather(landmarks, AXES, axis=0, tiled=True)
    all_spectral = lax.all_gather(spectral, AXES, axis=0, tiled=True)
    weights = pair_kernel(points, anchors)
    numer = jnp.dot(weights.astype(jnp.bfloat16), all_spectral, preferred_element_type=jnp.float32)
    coords = numer / jnp.sqrt(jnp.sum(weights, axis=1))[:, None] * math.sqrt(total)
    return (ortho, coords)


REDUNDANT_BYTES = 8 * 2**20


def solution(mesh):
    sizes = dict(mesh.shape)
    rows = sizes["row"]

    def run(landmarks, initial_basis, points):
        total = landmarks.shape[0]
        fits = 4 * total * total <= REDUNDANT_BYTES
        cube = sizes["grp"] == 4 and rows >= 4 and rows & (rows - 1) == 0
        spec = P(AXES, None)
        inner = jax.shard_map(
            fused_body if fits and cube else body,
            mesh=mesh,
            in_specs=(spec, spec, spec),
            out_specs=(spec, spec),
            check_vma=False,
        )
        return inner(landmarks, initial_basis, points)

    return run
```

```python
import functools
import math

import jax
import jax.numpy as jnp
from jax import lax
from jax.experimental import pallas as pl
from jax.experimental.pallas import tpu as pltpu
from jax.sharding import PartitionSpec as P

ITERS = 2
AXES = ("grp", "row")
spread = 0.25
LANES = 128
NN = (((1,), (0,)), ((), ()))
NT = (((1,), (1,)), ((), ()))
TN = (((0,), (0,)), ((), ()))
F32 = jnp.float32
BF16 = jnp.bfloat16

TOLERANCE = 0.06
START = 0.8
STEPS = (4, 3)
MORE = 16
CHUNK = 256
FILL = 512


def mm(a, b, dims):
    return lax.dot_general(a, b, dims, preferred_element_type=F32)


def split(x):
    high = x.astype(BF16)
    return high, (x - high.astype(F32)).astype(BF16)


def mm_split(a, b, dims):
    return mm(a[0], b[0], dims) + (mm(a[0], b[1], dims) + mm(a[1], b[0], dims))


def square_iota(n):
    return lax.broadcasted_iota(jnp.int32, (n, n), 0), lax.broadcasted_iota(jnp.int32, (n, n), 1)


def column_to_row(column):
    n = column.shape[0]
    i, j = square_iota(LANES)
    pieces = []
    for at in range(0, n, LANES):
        pieces.append(jnp.sum(jnp.where(i == j, column[at : at + LANES], 0.0), axis=0, keepdims=True))
    return jnp.concatenate(pieces, axis=1)


def row_squares(rows):
    wide = rows.astype(F32)
    return jnp.sum(wide * wide, axis=1, keepdims=True)


def direct_inverse(gram, work, unit):
    n = gram.shape[0]
    i, j = square_iota(n)
    row_at = lax.broadcasted_iota(jnp.int32, (n, 1), 0)
    work[...] = gram
    unit[...] = jnp.where(i == j, 1.0, 0.0)

    def step(k, pivots):
        row = work[pl.ds(k, 1), :]
        column = jnp.sum(jnp.where(j == k, work[...], 0.0), axis=1, keepdims=True)
        pivot = jnp.sum(jnp.where(row_at == k, column, 0.0), axis=0, keepdims=True)
        factor = jnp.where(row_at > k, column / pivot, 0.0)
        work[...] = work[...] - factor * row
        unit[...] = unit[...] - factor * unit[pl.ds(k, 1), :]
        return jnp.where(row_at == k, pivot, pivots)

    pivots = lax.fori_loop(0, n, step, jnp.ones((n, 1), F32))
    unit[...] = unit[...] / jnp.sqrt(pivots)


def scaled(gram):
    i, j = square_iota(gram.shape[0])
    diagonal = jnp.where(i == j, gram, 0.0)
    row_scale = lax.rsqrt(jnp.sum(diagonal, axis=0, keepdims=True)) * math.sqrt(START)
    column_scale = lax.rsqrt(jnp.sum(diagonal, axis=1, keepdims=True)) * math.sqrt(START)
    return gram * column_scale * row_scale, row_scale


def lower_half(n):
    i, j = square_iota(n)
    eye = jnp.where(i == j, 1.0, 0.0)
    return eye, jnp.where(i > j, 1.0, 0.5 * eye)


def polish(inverse, parts):
    n = inverse.shape[0]
    i, j = square_iota(n)
    eye, half = lower_half(n)
    mine = split(inverse)
    state = mm_split(split(mm_split(mine, parts, NN)), mine, NT)
    error = state - eye
    change = (error * half).astype(BF16)
    better = inverse - mm(change, inverse.astype(BF16), NN)
    signs = jnp.where(jnp.logical_and(i == j, better <= 0.0), 1.0, 0.0)
    return better, error * error + signs


def quick_inverse(gram, steps, fill):
    start, row_scale = scaled(gram)
    pair = split(start)
    eye, half = lower_half(gram.shape[0])
    state, inverse = start, eye
    for step in range(steps):
        change = (state - eye) * half
        low = change.astype(BF16)
        if step < steps - 1:
            left = state - mm(low, state.astype(BF16), NN)
            fill()
            state = left - mm(left.astype(BF16), low, NT)
        inverse = eye - change if step == 0 else inverse - mm(low, inverse.astype(BF16), NN)
    better, error = polish(inverse, pair)
    return better * row_scale, error


def safe_inverse(gram, out, work, corr):
    start, row_scale = scaled(gram)
    eye, _ = lower_half(gram.shape[0])
    corr[...] = start
    work[...] = eye

    def again(carry):
        better, error = polish(work[...], split(corr[...]))
        work[...] = better
        return carry[0] + 1, jnp.sum(error)

    def more(carry):
        return jnp.logical_and(carry[0] < MORE, jnp.logical_not(carry[1] < TOLERANCE**2))

    _, last = lax.while_loop(more, again, (0, jnp.float32(1.0)))
    out[...] = work[...] * row_scale

    @pl.when(jnp.logical_not(last < TOLERANCE**2))
    def _():
        direct_inverse(corr[...], work, out)
        out[...] = out[...] * row_scale


def stage_kernel(local_rows, mine, theirs, points, ortho_out, coords_out,
                 anchors, basis, kernel, affinity, weights, degrees, inverse, work, corr):
    width = points.shape[1]
    half_rows = mine.shape[0]
    total = 2 * half_rows
    count = points.shape[0]
    rank = inverse.shape[0]
    rate = math.log2(math.e) / (spread * width)
    for at, part in ((0, mine), (half_rows, theirs)):
        anchors[at : at + half_rows, :] = part[:, :width]
        basis[at : at + half_rows, :] = part[:, width:]
    squares = jnp.concatenate([row_squares(anchors[at : at + CHUNK, :]) for at in range(0, total, CHUNK)], axis=0) * rate
    squares_row = column_to_row(squares)
    sums = []
    for at in range(0, total, CHUNK):
        inner = mm(anchors[at : at + CHUNK, :], anchors[...], NT)
        value = jnp.exp2(inner * (2.0 * rate) - squares[at : at + CHUNK] - squares_row)
        kernel[at : at + CHUNK, :] = value
        sums.append(jnp.sum(value, axis=1, keepdims=True))
    scale = lax.rsqrt(jnp.concatenate(sums, axis=0))
    scale_row = column_to_row(scale)
    for at in range(0, total, CHUNK):
        affinity[at : at + CHUNK, :] = (kernel[at : at + CHUNK, :] * scale[at : at + CHUNK] * scale_row).astype(BF16)

    waiting = list(range(0, count, FILL))

    def fill():
        if waiting:
            at = waiting.pop(0)
            block = points[at : at + FILL, :]
            inner = mm(block, anchors[...], NT)
            value = jnp.exp2(inner * (2.0 * rate) - row_squares(block) * rate - squares_row)
            degrees[at : at + FILL, :] = jnp.sum(value, axis=1, keepdims=True)
            weights[at : at + FILL, :] = value.astype(BF16)

    def image_of(step, current):
        value = mm(basis[...], affinity[...], TN) if step == 0 else mm(current, affinity[...], NN)
        return split(value)

    def finish(ortho, lower):
        i, j = square_iota(rank)
        reciprocal = jnp.sum(jnp.where(i == j, lower, 0.0), axis=1, keepdims=True)
        spectral = (ortho * scale_row * reciprocal).astype(BF16)
        lanes = -(-local_rows // LANES) * LANES
        ortho_out[...] = jnp.transpose(ortho[:, 0:lanes])[0:local_rows, :]
        for at in range(0, count, FILL):
            numer = mm(weights[at : at + FILL, :], spectral, NT)
            coords_out[at : at + FILL, :] = numer * (lax.rsqrt(degrees[at : at + FILL, :]) * math.sqrt(total))

    current, faults = None, None
    for step in range(ITERS):
        parts = image_of(step, current)
        lower, error = quick_inverse(mm_split(parts, parts, NT), STEPS[min(step, len(STEPS) - 1)], fill)
        bad = jnp.sum(error, axis=0, keepdims=True)
        faults = bad if faults is None else jnp.maximum(faults, bad)
        faults = jnp.where(bad == bad, faults, bad)
        ortho = mm_split(split(lower), parts, NN)
        current = ortho.astype(BF16)
    while waiting:
        fill()
    finish(ortho, lower)
    fine = jnp.sum(faults) < TOLERANCE**2

    @pl.when(jnp.logical_not(fine))
    def _():
        current = None
        for step in range(ITERS):
            parts = image_of(step, current)
            safe_inverse(mm_split(parts, parts, NT), inverse, work, corr)
            ortho = mm_split(split(inverse[...]), parts, NN)
            current = ortho.astype(BF16)
        finish(ortho, inverse[...])


def stage(local_rows, mine, theirs, points):
    half_rows, wide = mine.shape
    count, width = points.shape
    rank = wide - width
    total = 2 * half_rows
    vmem = pl.BlockSpec(memory_space=pltpu.VMEM)
    return pl.pallas_call(
        functools.partial(stage_kernel, local_rows),
        out_shape=(jax.ShapeDtypeStruct((local_rows, rank), F32), jax.ShapeDtypeStruct((count, rank), F32)),
        in_specs=[vmem] * 3,
        out_specs=(vmem, vmem),
        scratch_shapes=[
            pltpu.VMEM((total, width), BF16),
            pltpu.VMEM((total, rank), BF16),
            pltpu.VMEM((total, total), F32),
            pltpu.VMEM((total, total), BF16),
            pltpu.VMEM((count, total), BF16),
            pltpu.VMEM((count, 1), F32),
            pltpu.VMEM((rank, rank), F32),
            pltpu.VMEM((rank, rank), F32),
            pltpu.VMEM((rank, rank), F32),
        ],
        compiler_params=pltpu.CompilerParams(vmem_limit_bytes=36 * 2**20),
    )(mine, theirs, points)


def squared_rows(rows):
    return jnp.sum(jnp.square(rows.astype(jnp.float32)), axis=1)


def pair_kernel(left, right):
    inner = lax.dot_general(
        left, right, (((1,), (1,)), ((), ())), preferred_element_type=jnp.float32
    )
    dist = squared_rows(left)[:, None] + squared_rows(right)[None, :] - 2.0 * inner
    return jnp.exp(-dist / (spread * left.shape[1]))


def exchange(value, mask):
    count = lax.axis_size("grp") * lax.axis_size("row")
    return lax.ppermute(value, AXES, [(i, i ^ mask) for i in range(count)])


def gather_relative(own):
    rows = lax.axis_size("row")
    near, partner, across = 1, rows, 2 * rows
    parts = [own] + [exchange(own, mask) for mask in range(2, rows, 2)]
    half = len(parts) // 2
    first = jnp.concatenate(parts[:half], axis=0)
    second = jnp.concatenate(parts[half:], axis=0)
    first_near = exchange(first, near)
    second_across = exchange(second, across)
    first_pair = jnp.concatenate([first, first_near], axis=0)
    second_pair = jnp.concatenate([second, second_across], axis=0)
    first_rest = exchange(first_pair, across)
    second_rest = exchange(second_pair, near)
    mine = jnp.concatenate([first_pair, second_pair, first_rest, second_rest], axis=0)
    return mine, exchange(mine, partner)


def fused_body(landmarks, initial_basis, points):
    own = lax.optimization_barrier(jnp.concatenate([landmarks, initial_basis], axis=1))
    mine, theirs = gather_relative(own)
    return stage(landmarks.shape[0], mine, theirs, points)


def body(landmarks, initial_basis, points):
    local_rows = landmarks.shape[0]
    total = local_rows * lax.axis_size("grp") * lax.axis_size("row")
    row_index = lax.axis_index("row")
    group_rows = lax.all_gather(landmarks, "row", axis=0, tiled=True)
    cross_rows = lax.all_gather(landmarks, "grp", axis=0, tiled=True)
    land_kernel = pair_kernel(group_rows, cross_rows)
    group_degree = lax.psum(jnp.sum(land_kernel, axis=1), "row")
    own_degree = lax.dynamic_slice_in_dim(group_degree, row_index * local_rows, local_rows, 0)
    cross_degree = lax.psum(jnp.sum(land_kernel, axis=0), "grp")
    row_scale = 1.0 / jnp.sqrt(group_degree)
    column_scale = 1.0 / jnp.sqrt(cross_degree)
    affinity = (land_kernel * row_scale[:, None] * column_scale[None, :]).astype(jnp.bfloat16)
    current = initial_basis
    for step in range(ITERS):
        cross_basis = lax.all_gather(current, "grp", axis=0, tiled=True)
        image = lax.psum_scatter(
            jnp.dot(affinity, cross_basis, preferred_element_type=jnp.float32),
            "row",
            scatter_dimension=0,
            tiled=True,
        )
        gram = lax.psum(jnp.dot(image.T, image, precision=lax.Precision.HIGHEST), ("grp", "row"))
        lower = jnp.linalg.cholesky(gram)
        ortho = jax.scipy.linalg.solve_triangular(lower, image.T, lower=True).T
        current = ortho.astype(jnp.bfloat16)
    lam = jnp.diagonal(lower)
    own_scale = 1.0 / jnp.sqrt(own_degree)
    spectral = (ortho * own_scale[:, None] / lam[None, :]).astype(jnp.bfloat16)
    anchors = lax.all_gather(landmarks, AXES, axis=0, tiled=True)
    all_spectral = lax.all_gather(spectral, AXES, axis=0, tiled=True)
    weights = pair_kernel(points, anchors)
    numer = jnp.dot(weights.astype(jnp.bfloat16), all_spectral, preferred_element_type=jnp.float32)
    coords = numer / jnp.sqrt(jnp.sum(weights, axis=1))[:, None] * math.sqrt(total)
    return (ortho, coords)


REDUNDANT_BYTES = 8 * 2**20


def solution(mesh):
    sizes = dict(mesh.shape)
    rows = sizes["row"]

    def run(landmarks, initial_basis, points):
        total = landmarks.shape[0]
        fits = 4 * total * total <= REDUNDANT_BYTES
        cube = sizes["grp"] == 4 and rows >= 4 and rows & (rows - 1) == 0
        spec = P(AXES, None)
        inner = jax.shard_map(
            fused_body if fits and cube else body,
            mesh=mesh,
            in_specs=(spec, spec, spec),
            out_specs=(spec, spec),
            check_vma=False,
        )
        return inner(landmarks, initial_basis, points)

    return run
```

```python
import functools
import math

import jax
import jax.numpy as jnp
from jax import lax
from jax.experimental import pallas as pl
from jax.experimental.pallas import tpu as pltpu
from jax.sharding import PartitionSpec as P

ITERS = 2
AXES = ("grp", "row")
spread = 0.25
LANES = 128
NN = (((1,), (0,)), ((), ()))
NT = (((1,), (1,)), ((), ()))
TN = (((0,), (0,)), ((), ()))
F32 = jnp.float32
BF16 = jnp.bfloat16

TOLERANCE = 0.06
START = 0.8
STEPS = (4, 3)
MORE = 16
CHUNK = 256
FILL = 512


def mm(a, b, dims):
    return lax.dot_general(a, b, dims, preferred_element_type=F32)


def split(x):
    high = x.astype(BF16)
    return high, (x - high.astype(F32)).astype(BF16)


def mm_split(a, b, dims):
    return mm(a[0], b[0], dims) + (mm(a[0], b[1], dims) + mm(a[1], b[0], dims))


def square_iota(n):
    return lax.broadcasted_iota(jnp.int32, (n, n), 0), lax.broadcasted_iota(jnp.int32, (n, n), 1)


def column_to_row(column):
    n = column.shape[0]
    i, j = square_iota(LANES)
    pieces = []
    for at in range(0, n, LANES):
        pieces.append(jnp.sum(jnp.where(i == j, column[at : at + LANES], 0.0), axis=0, keepdims=True))
    return jnp.concatenate(pieces, axis=1)


def row_squares(rows):
    wide = rows.astype(F32)
    return jnp.sum(wide * wide, axis=1, keepdims=True)


def direct_inverse(gram, work, unit):
    n = gram.shape[0]
    i, j = square_iota(n)
    row_at = lax.broadcasted_iota(jnp.int32, (n, 1), 0)
    work[...] = gram
    unit[...] = jnp.where(i == j, 1.0, 0.0)

    def step(k, pivots):
        row = work[pl.ds(k, 1), :]
        column = jnp.sum(jnp.where(j == k, work[...], 0.0), axis=1, keepdims=True)
        pivot = jnp.sum(jnp.where(row_at == k, column, 0.0), axis=0, keepdims=True)
        factor = jnp.where(row_at > k, column / pivot, 0.0)
        work[...] = work[...] - factor * row
        unit[...] = unit[...] - factor * unit[pl.ds(k, 1), :]
        return jnp.where(row_at == k, pivot, pivots)

    pivots = lax.fori_loop(0, n, step, jnp.ones((n, 1), F32))
    unit[...] = unit[...] / jnp.sqrt(pivots)


def scaled(gram):
    i, j = square_iota(gram.shape[0])
    diagonal = jnp.where(i == j, gram, 0.0)
    row_scale = lax.rsqrt(jnp.sum(diagonal, axis=0, keepdims=True)) * math.sqrt(START)
    column_scale = lax.rsqrt(jnp.sum(diagonal, axis=1, keepdims=True)) * math.sqrt(START)
    return gram * column_scale * row_scale, row_scale


def lower_half(n):
    i, j = square_iota(n)
    eye = jnp.where(i == j, 1.0, 0.0)
    return eye, jnp.where(i > j, 1.0, 0.5 * eye)


def polish(inverse, parts):
    n = inverse.shape[0]
    i, j = square_iota(n)
    eye, half = lower_half(n)
    mine = split(inverse)
    state = mm_split(split(mm_split(mine, parts, NN)), mine, NT)
    error = state - eye
    change = (error * half).astype(BF16)
    better = inverse - mm(change, inverse.astype(BF16), NN)
    signs = jnp.where(jnp.logical_and(i == j, better <= 0.0), 1.0, 0.0)
    return better, error * error + signs


def quick_inverse(gram, steps):
    start, row_scale = scaled(gram)
    pair = split(start)
    eye, half = lower_half(gram.shape[0])
    state, inverse = start, eye
    for step in range(steps):
        change = (state - eye) * half
        low = change.astype(BF16)
        if step < steps - 1:
            left = state - mm(low, state.astype(BF16), NN)
            state = left - mm(left.astype(BF16), low, NT)
        inverse = eye - change if step == 0 else inverse - mm(low, inverse.astype(BF16), NN)
    better, error = polish(inverse, pair)
    return better * row_scale, error


def safe_inverse(gram, out, work, corr):
    start, row_scale = scaled(gram)
    eye, _ = lower_half(gram.shape[0])
    corr[...] = start
    work[...] = eye

    def again(carry):
        better, error = polish(work[...], split(corr[...]))
        work[...] = better
        return carry[0] + 1, jnp.sum(error)

    def more(carry):
        return jnp.logical_and(carry[0] < MORE, jnp.logical_not(carry[1] < TOLERANCE**2))

    _, last = lax.while_loop(more, again, (0, jnp.float32(1.0)))
    out[...] = work[...] * row_scale

    @pl.when(jnp.logical_not(last < TOLERANCE**2))
    def _():
        direct_inverse(corr[...], work, out)
        out[...] = out[...] * row_scale


def rate_of(width):
    return math.log2(math.e) / (spread * width)


def point_part(points, at, rows, anchors, squares_row, point_squares, weights, width):
    inner = mm(points[at : at + rows, :], anchors, NT)
    value = jnp.exp2(inner * (2.0 * rate_of(width)) - point_squares - squares_row)
    weights[at : at + rows, :] = value.astype(BF16)
    return jnp.sum(value, axis=1, keepdims=True)


def squares_of(anchors, width):
    total = anchors.shape[0]
    pieces = [row_squares(anchors[at : at + CHUNK, :]) for at in range(0, total, CHUNK)]
    return jnp.concatenate(pieces, axis=0) * rate_of(width)


def early_kernel(mine, theirs, points, kernel, weights, degrees, point_squares, anchors):
    width = points.shape[1]
    part = mine.shape[0]
    total = 2 * part
    anchors[0:part, :] = mine[:, :width]
    anchors[part:total, :] = theirs[:, :width]
    squares = squares_of(anchors, width)
    squares_row = column_to_row(squares)
    for at in range(0, total, CHUNK):
        inner = mm(anchors[at : at + CHUNK, :], anchors[...], NT)
        kernel[at : at + CHUNK, :] = jnp.exp2(inner * (2.0 * rate_of(width)) - squares[at : at + CHUNK] - squares_row)
    for at in range(0, points.shape[0], FILL):
        own = row_squares(points[at : at + FILL, :]) * rate_of(width)
        point_squares[at : at + FILL, :] = own
        degrees[at : at + FILL, :] = point_part(points, at, FILL, anchors[...], squares_row, own, weights, width)


def late_kernel(local_rows, mine, theirs, mine_rest, theirs_rest, points, kernel_early, weights_early, degrees_early,
                point_squares, ortho_out, coords_out,
                anchors, basis, kernel, affinity, weights, inverse, work, corr):
    width = points.shape[1]
    part = mine.shape[0]
    total = 4 * part
    half = 2 * part
    count = points.shape[0]
    rank = inverse.shape[0]
    for at, block in enumerate((mine, theirs, mine_rest, theirs_rest)):
        anchors[at * part : (at + 1) * part, :] = block[:, :width]
        basis[at * part : (at + 1) * part, :] = block[:, width:]
    squares = squares_of(anchors, width)
    squares_row = column_to_row(squares)
    sums = [None] * (total // CHUNK)
    for at in range(half, total, CHUNK):
        inner = mm(anchors[at : at + CHUNK, :], anchors[...], NT)
        value = jnp.exp2(inner * (2.0 * rate_of(width)) - squares[at : at + CHUNK] - squares_row)
        kernel[at : at + CHUNK, :] = value
        sums[at // CHUNK] = jnp.sum(value, axis=1, keepdims=True)
        kernel[0:half, at : at + CHUNK] = jnp.transpose(value[:, 0:half])
    for at in range(0, half, CHUNK):
        own = kernel_early[at : at + CHUNK, :]
        kernel[at : at + CHUNK, 0:half] = own
        rest = kernel[at : at + CHUNK, half:total]
        sums[at // CHUNK] = jnp.sum(own, axis=1, keepdims=True) + jnp.sum(rest, axis=1, keepdims=True)
    scale = lax.rsqrt(jnp.concatenate(sums, axis=0))
    scale_row = column_to_row(scale)
    for at in range(0, total, CHUNK):
        affinity[at : at + CHUNK, :] = (kernel[at : at + CHUNK, :] * scale[at : at + CHUNK] * scale_row).astype(BF16)

    def image_of(step, current):
        value = mm(basis[...], affinity[...], TN) if step == 0 else mm(current, affinity[...], NN)
        return split(value)

    def finish(ortho, lower, degrees):
        i, j = square_iota(rank)
        reciprocal = jnp.sum(jnp.where(i == j, lower, 0.0), axis=1, keepdims=True)
        spectral = (ortho * scale_row * reciprocal).astype(BF16)
        lanes = -(-local_rows // LANES) * LANES
        ortho_out[...] = jnp.transpose(ortho[:, 0:lanes])[0:local_rows, :]
        for at, degree in zip(range(0, count, FILL), degrees):
            numer = mm(weights_early[at : at + FILL, :], spectral[:, 0:half], NT)
            numer = numer + mm(weights[at : at + FILL, :], spectral[:, half:total], NT)
            coords_out[at : at + FILL, :] = numer * (lax.rsqrt(degree) * math.sqrt(total))

    degrees = []
    for at in range(0, count, FILL):
        more = point_part(points, at, FILL, anchors[half:total, :], squares_row[:, half:total],
                          point_squares[at : at + FILL, :], weights, width)
        degrees.append(degrees_early[at : at + FILL, :] + more)
    current, faults = None, None
    for step in range(ITERS):
        parts = image_of(step, current)
        lower, error = quick_inverse(mm_split(parts, parts, NT), STEPS[min(step, len(STEPS) - 1)])
        bad = jnp.sum(error, axis=0, keepdims=True)
        faults = bad if faults is None else jnp.where(jnp.logical_and(faults == faults, bad < faults), faults, bad)
        ortho = mm_split(split(lower), parts, NN)
        current = ortho.astype(BF16)
    finish(ortho, lower, degrees)
    fine = jnp.sum(faults) < TOLERANCE**2

    @pl.when(jnp.logical_not(fine))
    def _():
        current = None
        for step in range(ITERS):
            parts = image_of(step, current)
            safe_inverse(mm_split(parts, parts, NT), inverse, work, corr)
            ortho = mm_split(split(inverse[...]), parts, NN)
            current = ortho.astype(BF16)
        finish(ortho, inverse[...], degrees)


def early(mine, theirs, points):
    part, wide = mine.shape
    count, width = points.shape
    total = 2 * part
    vmem = pl.BlockSpec(memory_space=pltpu.VMEM)
    return pl.pallas_call(
        early_kernel,
        out_shape=(
            jax.ShapeDtypeStruct((total, total), F32),
            jax.ShapeDtypeStruct((count, total), BF16),
            jax.ShapeDtypeStruct((count, 1), F32),
            jax.ShapeDtypeStruct((count, 1), F32),
        ),
        in_specs=[vmem] * 3,
        out_specs=(vmem,) * 4,
        scratch_shapes=[pltpu.VMEM((total, width), BF16)],
        compiler_params=pltpu.CompilerParams(vmem_limit_bytes=24 * 2**20),
        cost_estimate=pl.CostEstimate(
            flops=2 * total * width * (total + count), transcendentals=total * (total + count), bytes_accessed=4 * count * width
        ),
    )(mine, theirs, points)


def late(local_rows, mine, theirs, mine_rest, theirs_rest, points, found):
    part, wide = mine.shape
    count, width = points.shape
    rank = wide - width
    total = 4 * part
    vmem = pl.BlockSpec(memory_space=pltpu.VMEM)
    return pl.pallas_call(
        functools.partial(late_kernel, local_rows),
        out_shape=(jax.ShapeDtypeStruct((local_rows, rank), F32), jax.ShapeDtypeStruct((count, rank), F32)),
        in_specs=[vmem] * 9,
        out_specs=(vmem, vmem),
        scratch_shapes=[
            pltpu.VMEM((total, width), BF16),
            pltpu.VMEM((total, rank), BF16),
            pltpu.VMEM((total, total), F32),
            pltpu.VMEM((total, total), BF16),
            pltpu.VMEM((count, total // 2), BF16),
            pltpu.VMEM((rank, rank), F32),
            pltpu.VMEM((rank, rank), F32),
            pltpu.VMEM((rank, rank), F32),
        ],
        compiler_params=pltpu.CompilerParams(vmem_limit_bytes=36 * 2**20),
    )(mine, theirs, mine_rest, theirs_rest, points, *found)


def squared_rows(rows):
    return jnp.sum(jnp.square(rows.astype(jnp.float32)), axis=1)


def pair_kernel(left, right):
    inner = lax.dot_general(
        left, right, (((1,), (1,)), ((), ())), preferred_element_type=jnp.float32
    )
    dist = squared_rows(left)[:, None] + squared_rows(right)[None, :] - 2.0 * inner
    return jnp.exp(-dist / (spread * left.shape[1]))


def exchange(value, mask):
    count = lax.axis_size("grp") * lax.axis_size("row")
    return lax.ppermute(value, AXES, [(i, i ^ mask) for i in range(count)])


def fused_body(landmarks, initial_basis, points):
    rows = lax.axis_size("row")
    near, partner, across = 1, rows, 2 * rows
    own = lax.optimization_barrier(jnp.concatenate([landmarks, initial_basis], axis=1))
    parts = [own] + [exchange(own, mask) for mask in range(2, rows, 2)]
    half = len(parts) // 2
    first = jnp.concatenate(parts[:half], axis=0)
    second = jnp.concatenate(parts[half:], axis=0)
    first_near = exchange(first, near)
    second_across = exchange(second, across)
    first_pair = jnp.concatenate([first, first_near], axis=0)
    second_pair = jnp.concatenate([second, second_across], axis=0)
    first_rest = exchange(first_pair, across)
    second_rest = exchange(second_pair, near)
    mine = jnp.concatenate([first_pair, second_pair], axis=0)
    theirs = exchange(mine, partner)
    found = early(mine, theirs, points)
    first_rest, second_rest, found = lax.optimization_barrier((first_rest, second_rest, found))
    mine_rest = jnp.concatenate([first_rest, second_rest], axis=0)
    theirs_rest = exchange(mine_rest, partner)
    return late(landmarks.shape[0], mine, theirs, mine_rest, theirs_rest, points, found)


def body(landmarks, initial_basis, points):
    local_rows = landmarks.shape[0]
    total = local_rows * lax.axis_size("grp") * lax.axis_size("row")
    row_index = lax.axis_index("row")
    group_rows = lax.all_gather(landmarks, "row", axis=0, tiled=True)
    cross_rows = lax.all_gather(landmarks, "grp", axis=0, tiled=True)
    land_kernel = pair_kernel(group_rows, cross_rows)
    group_degree = lax.psum(jnp.sum(land_kernel, axis=1), "row")
    own_degree = lax.dynamic_slice_in_dim(group_degree, row_index * local_rows, local_rows, 0)
    cross_degree = lax.psum(jnp.sum(land_kernel, axis=0), "grp")
    row_scale = 1.0 / jnp.sqrt(group_degree)
    column_scale = 1.0 / jnp.sqrt(cross_degree)
    affinity = (land_kernel * row_scale[:, None] * column_scale[None, :]).astype(jnp.bfloat16)
    current = initial_basis
    for step in range(ITERS):
        cross_basis = lax.all_gather(current, "grp", axis=0, tiled=True)
        image = lax.psum_scatter(
            jnp.dot(affinity, cross_basis, preferred_element_type=jnp.float32),
            "row",
            scatter_dimension=0,
            tiled=True,
        )
        gram = lax.psum(jnp.dot(image.T, image, precision=lax.Precision.HIGHEST), ("grp", "row"))
        lower = jnp.linalg.cholesky(gram)
        ortho = jax.scipy.linalg.solve_triangular(lower, image.T, lower=True).T
        current = ortho.astype(jnp.bfloat16)
    lam = jnp.diagonal(lower)
    own_scale = 1.0 / jnp.sqrt(own_degree)
    spectral = (ortho * own_scale[:, None] / lam[None, :]).astype(jnp.bfloat16)
    anchors = lax.all_gather(landmarks, AXES, axis=0, tiled=True)
    all_spectral = lax.all_gather(spectral, AXES, axis=0, tiled=True)
    weights = pair_kernel(points, anchors)
    numer = jnp.dot(weights.astype(jnp.bfloat16), all_spectral, preferred_element_type=jnp.float32)
    coords = numer / jnp.sqrt(jnp.sum(weights, axis=1))[:, None] * math.sqrt(total)
    return (ortho, coords)


REDUNDANT_BYTES = 8 * 2**20


def solution(mesh):
    sizes = dict(mesh.shape)
    rows = sizes["row"]

    def run(landmarks, initial_basis, points):
        total = landmarks.shape[0]
        fits = 4 * total * total <= REDUNDANT_BYTES
        cube = sizes["grp"] == 4 and rows >= 4 and rows & (rows - 1) == 0
        spec = P(AXES, None)
        inner = jax.shard_map(
            fused_body if fits and cube else body,
            mesh=mesh,
            in_specs=(spec, spec, spec),
            out_specs=(spec, spec),
            check_vma=False,
        )
        return inner(landmarks, initial_basis, points)

    return run
```
